512 devices in a mesh: ctx: 16 (over z_lo, core), exp: 32 (over x, z_hi, y).
Axes of the slice: x: 4, y: 4, z: 16 (z_hi: 2, z_lo: 8; z = z_hi * 8 + z_lo), core: 2. Of those that a mesh axis runs over, the one named last changes fastest.
Arguments:
- queries: bfloat16 [32, 2048, 2048], P('exp', 'ctx'), may hold values from -8 to 8
- key_states: bfloat16 [32, 2048, 256], P('exp', 'ctx'), may hold values from -4 to 4
- value_states: bfloat16 [32, 2048, 256], P('exp', 'ctx'), may hold values from -6 to 6
- residual: bfloat16 [32, 2048, 2048], P('exp', 'ctx'), may hold values from -25 to 25
- norm_gain: float32 [2048], replicated, may hold values from 0.1 to 1.9
- expert_ids: int32 [32, 2048, 8], P('exp', 'ctx'), may hold values from 0 to 127, as said below
- gate_weights: float32 [32, 2048, 8], P('exp', 'ctx'), may hold values from 0.2 to 1
- expert_in: bfloat16 [32, 2048, 384], P('exp'), may hold values from -0.125 to 0.125
- expert_out: bfloat16 [32, 192, 2048], P('exp'), may hold values from -0.4375 to 0.4375
Outputs:
- attention: bfloat16 [32, 2048, 2048], P('exp', 'ctx')
- expert_mix: bfloat16 [32, 2048, 2048], P('exp', 'ctx')
The draws below stay inside these ranges and needn't reach their ends.
Inputs may be any that keep to these rules, and one draw needn't show every extreme that they name: `expert_ids`: experts 0 to 7 are the experts in flight. Each row names 8 different experts. Among the rows of one device (an aligned block of 128 positions of a prompt) no expert in flight is named by more than 16 rows, and one expert in flight, the same for that block in every prompt, is named by exactly 16 rows.
All inputs are finite; a program needn't handle non-finite values.
Results may differ from the reference program's by a relative error of at most 0.02.
Values may be sent and summed in bfloat16 or wider, within the bound.
A program may use at most 64 MiB of HBM per device.

```python
import math
import jax
import jax.numpy as jnp
from jax import lax

D = 2048
HEADS = 16
KV_HEADS = 2
HD = 128
EXPERTS = 128
TOPK = 8
SPLIT = 4
TOK_DEV = 128
HID_DEV = 192
FLIGHT = 8
CAP = 16
PROMPTS = 32
SEQ = 2048


def drawn_pair(key):
    query_seed = jax.random.fold_in(key, 11)
    key_seed = jax.random.fold_in(key, 12)
    queries = jnp.clip(jax.random.normal(query_seed, (PROMPTS, SEQ, HEADS, HD), jnp.float32), -4.0, 4.0) * 2.0
    key_values = jnp.clip(jax.random.normal(key_seed, (PROMPTS, SEQ, KV_HEADS, HD), jnp.float32), -4.0, 4.0)
    return (queries.reshape(PROMPTS, SEQ, HEADS * HD), key_values.reshape(PROMPTS, SEQ, KV_HEADS * HD))


def draw_queries(key, part):
    return drawn_pair(key)[0].astype(jnp.bfloat16)


def draw_key_states(key, part):
    return drawn_pair(key)[1].astype(jnp.bfloat16)


def draw_residual(key, part):
    noise_seed = jax.random.fold_in(key, 21)
    row_seed = jax.random.fold_in(key, 22)
    column_seed = jax.random.fold_in(key, 23)
    sample = jnp.clip(jax.random.normal(noise_seed, (PROMPTS, SEQ, D), jnp.float32), -4.0, 4.0)
    log_low = math.log(0.4)
    log_high = math.log(2.5)
    row_scale = jnp.exp(jax.random.uniform(row_seed, (PROMPTS, SEQ, 1), jnp.float32, log_low, log_high))
    column_scale = jnp.exp(jax.random.uniform(column_seed, (D,), jnp.float32, log_low, log_high))
    return (sample * row_scale * column_scale).astype(jnp.bfloat16)


def draw_expert_ids(key, part):
    id_seed = jax.random.fold_in(key, 31)
    seed_list = jax.random.split(id_seed, 6)
    block_count = SEQ // TOK_DEV
    others_count = EXPERTS - FLIGHT
    first_draw = jax.random.randint(seed_list[0], (PROMPTS, block_count, FLIGHT), 0, CAP + 1)
    second_draw = jax.random.randint(seed_list[1], (PROMPTS, block_count, FLIGHT), 0, CAP + 1)
    load_counts = first_draw * second_draw // CAP
    busiest = jax.random.randint(seed_list[2], (block_count,), 0, FLIGHT)
    travelling_ids = jnp.arange(FLIGHT, dtype=jnp.int32)
    load_counts = jnp.where(travelling_ids[None, None, :] == busiest[None, :, None], CAP, load_counts)
    row_ids = jnp.arange(TOK_DEV, dtype=jnp.int32)
    priority = jax.random.randint(seed_list[3], (PROMPTS, block_count, FLIGHT, TOK_DEV), 0, 1 << 20) * TOK_DEV + row_ids
    ranking = jnp.argsort(jnp.argsort(priority, axis=-1), axis=-1)
    chosen_slots = ranking < load_counts[..., None]
    travelling_rows = jnp.transpose(chosen_slots, (0, 1, 3, 2)).astype(jnp.int32)
    travelling_count = jnp.sum(travelling_rows, axis=-1)
    travelling_rank = jnp.cumsum(travelling_rows, axis=-1) - 1
    slot_numbers = jnp.arange(TOPK, dtype=jnp.int32)
    travelling_place = jnp.sum(jnp.where((travelling_rows[..., None] == 1) & (travelling_rank[..., None] == slot_numbers), travelling_ids[:, None], 0), axis=-2)
    other_priority = jax.random.randint(seed_list[4], (PROMPTS, block_count, TOK_DEV, others_count), 0, 1 << 20) * others_count + jnp.arange(others_count, dtype=jnp.int32)
    other_ids = lax.top_k(other_priority, TOPK)[1] + FLIGHT
    shifted_rows = slot_numbers - travelling_count[..., None]
    other_place = jnp.sum(jnp.where(slot_numbers[:, None] == shifted_rows[..., None, :], other_ids[..., :, None], 0), axis=-2)
    selected_rows = jnp.where(slot_numbers < travelling_count[..., None], travelling_place, other_place)
    shuffle = jnp.argsort(jax.random.randint(seed_list[5], (PROMPTS, block_count, TOK_DEV, TOPK), 0, 1 << 20) * TOPK + slot_numbers, axis=-1)
    selected_rows = jnp.take_along_axis(selected_rows, shuffle, axis=-1)
    return selected_rows.reshape(PROMPTS, SEQ, TOPK).astype(jnp.int32)


def steps_of(key, dims, shards, low, top_value):
    factor_of = 1.0
    for position, blocks in shards:
        draws = jax.random.uniform(jax.random.fold_in(jax.random.fold_in(key, 6), position), (blocks,), jnp.float32, low / len(shards), top_value / len(shards))
        factor_of = factor_of * jnp.repeat(jnp.exp(draws), dims[position] // blocks).reshape((-1,) + (1,) * (len(dims) - 1 - position))
    return factor_of


def gaussian(own_key, extent, deviation, bound, cuts=(), kind=jnp.bfloat16):
    array = jax.random.normal(own_key, extent, jnp.float32) * deviation
    if len(cuts) > 0:
        array = steps_of(own_key, extent, cuts, -0.22, 0.18) * array
    return jnp.clip(array, min=-bound, max=bound).astype(kind)


def setup_inputs(seed: int = 0) -> dict:
    key_of = jax.random.split(jax.random.key(seed), 10)
    queries = draw_queries(jax.random.fold_in(key_of[9], 71), 0)
    key_states = draw_key_states(jax.random.fold_in(key_of[9], 71), 0)
    value_states = gaussian(key_of[2], (PROMPTS, SEQ, KV_HEADS * HD), 1.0, 6.0, ((0, 32), (1, 16)))
    residual = draw_residual(jax.random.fold_in(key_of[9], 71), 0)
    norm_gain = jnp.clip(1.0 + 0.18 * jax.random.normal(key_of[4], (D,), jnp.float32), 0.1, 1.9)
    expert_ids = draw_expert_ids(jax.random.fold_in(key_of[9], 71), 0)
    gate_weights = jnp.clip(0.2 + 0.8 * jax.random.uniform(key_of[6], (PROMPTS, SEQ, TOPK), jnp.float32) ** steps_of(key_of[6], (PROMPTS, SEQ, TOPK), ((0, 32), (1, 16)), -0.2, 0.2), 0.2, 1.0)
    expert_in = gaussian(key_of[7], (FLIGHT * SPLIT, D, 2 * HID_DEV), D ** -0.5, 0.125, ((0, 32),))
    expert_out = gaussian(key_of[8], (FLIGHT * SPLIT, HID_DEV, D), HID_DEV ** -0.5, 0.4375, ((0, 32),))
    return dict(queries=queries, key_states=key_states, value_states=value_states, residual=residual, norm_gain=norm_gain, expert_ids=expert_ids, gate_weights=gate_weights, expert_in=expert_in, expert_out=expert_out)


norm_epsilon = 1e-06
masked_score = -1e+30

def prompt_attention(operands):
    prompt_queries, prompt_keys, prompt_values = operands
    group_size = HEADS // KV_HEADS
    block_rows = math.gcd(SEQ, 512)
    score_scale = 1.0 / math.sqrt(HD)
    query_blocks = prompt_queries.reshape(SEQ // block_rows, block_rows, KV_HEADS, group_size, HD)
    keys_wide = prompt_keys.reshape(SEQ, KV_HEADS, HD).astype(jnp.float32)
    values_wide = prompt_values.reshape(SEQ, KV_HEADS, HD).astype(jnp.float32)
    key_spots = jnp.arange(SEQ, dtype=jnp.int32)
    block_starts = jnp.arange(SEQ // block_rows, dtype=jnp.int32) * block_rows

    def one_block(block_item):
        query_block, block_start = block_item
        query_spots = block_start + jnp.arange(block_rows, dtype=jnp.int32)
        scores = jnp.einsum('qhgd,khd->qhgk', query_block.astype(jnp.float32), keys_wide) * score_scale
        allowed = (key_spots[None, :] <= query_spots[:, None])[:, None, None, :]
        scores = jnp.where(allowed, scores, masked_score)
        row_top = lax.optimization_barrier(jnp.max(scores, axis=-1, keepdims=True))
        raised = jnp.where(allowed, jnp.exp(scores - row_top), 0.0)
        denominator = lax.optimization_barrier(jnp.sum(raised, axis=-1))
        rounded = lax.optimization_barrier(raised.astype(jnp.bfloat16)).astype(jnp.float32)
        output = jnp.einsum('qhgk,khd->qhgd', rounded, values_wide) / denominator[..., None]
        return output.astype(jnp.bfloat16).reshape(block_rows, HEADS * HD)
    return lax.map(one_block, (query_blocks, block_starts)).reshape(SEQ, HEADS * HD)

def expert_reference(residual, attention, norm_gain, expert_ids, gate_weights, expert_in, expert_out):
    block_count = PROMPTS * (SEQ // TOK_DEV)
    hidden = residual.reshape(block_count, TOK_DEV, D).astype(jnp.float32) + attention.reshape(block_count, TOK_DEV, D).astype(jnp.float32)
    normed = (hidden * lax.rsqrt(lax.optimization_barrier(jnp.mean(hidden * hidden, axis=-1, keepdims=True)) + norm_epsilon) * norm_gain).astype(jnp.bfloat16)
    normed_wide = normed.astype(jnp.float32)
    picked = expert_ids.reshape(block_count, TOK_DEV, TOPK)
    gate_rows = gate_weights.reshape(block_count, TOK_DEV, TOPK)
    slot_numbers = jnp.arange(CAP, dtype=jnp.int32)

    def per_expert(mixture, expert):
        matches = picked == expert
        member_count = lax.optimization_barrier(jnp.sum(matches.astype(jnp.int32), axis=-1))
        route_weight = lax.optimization_barrier(jnp.sum(jnp.where(matches, gate_rows, 0.0), axis=-1))
        slot_rank = jnp.cumsum(member_count, axis=1) - member_count
        chosen_slots = (member_count[:, None, :] == 1) & (slot_rank[:, None, :] == slot_numbers[None, :, None])
        selector = jnp.where(chosen_slots, 1.0, 0.0).astype(jnp.float32)
        gathered = jnp.einsum('bct,btd->bcd', selector, normed_wide).astype(jnp.bfloat16).reshape(block_count * CAP, D)
        combined = jnp.zeros((block_count * CAP, D), jnp.float32)
        for quarter in range(SPLIT):
            holder = expert * SPLIT + quarter
            weight_in = lax.dynamic_index_in_dim(expert_in, holder, 0, keepdims=False)
            weight_out = lax.dynamic_index_in_dim(expert_out, holder, 0, keepdims=False)
            projected = jnp.dot(gathered, weight_in, preferred_element_type=jnp.float32)
            activated = (jax.nn.silu(projected[:, :HID_DEV]) * projected[:, HID_DEV:]).astype(jnp.bfloat16)
            share_out = jnp.dot(activated, weight_out, preferred_element_type=jnp.float32)
            combined = combined + lax.optimization_barrier(share_out.astype(jnp.bfloat16)).astype(jnp.float32)
        scaled = jnp.where(chosen_slots, route_weight[:, None, :], 0.0)
        mixture = mixture + jnp.einsum('bct,bcd->btd', scaled, combined.reshape(block_count, CAP, D), precision=lax.Precision.HIGHEST)
        return (mixture, None)
    mixture = lax.scan(per_expert, jnp.zeros((block_count, TOK_DEV, D), jnp.float32), jnp.arange(FLIGHT, dtype=jnp.int32))[0]
    return mixture.astype(jnp.bfloat16).reshape(PROMPTS, SEQ, D)

def reference(queries, key_states, value_states, residual, norm_gain, expert_ids, gate_weights, expert_in, expert_out):
    attention = lax.map(prompt_attention, (queries, key_states, value_states))
    expert_mix = expert_reference(residual, attention, norm_gain, expert_ids, gate_weights, expert_in, expert_out)
    return (attention, expert_mix)
```

```python
import functools
import math

import jax
import jax.numpy as jnp
from jax import lax
from jax.experimental import pallas as pl
from jax.experimental.pallas import tpu as pltpu
from jax.sharding import PartitionSpec as P

D = 2048
HEADS = 16
KV_HEADS = 2
HD = 128
TOK = 128
CAP = 16
HID = 192
PLANES = 8
SUBS = 16
IN_ROWS = 1024 // SUBS
OUT_SUBS = 6
OUT_ROWS = 16
EPSILON = 1e-06
MASKED = -1e30
MESH = pl.DeviceIdType.MESH
NEAR_FIRST = ((0, 0), (0, 1), (1, 0), (3, 0), (1, 1), (3, 1), (2, 0), (2, 1))


def device(plane, core, x, half, y):
    return (plane * 2 + core, x * 8 + half * 4 + y)


def transposed_dot(a, b):
    return lax.dot_general(a, b, (((0,), (0,)), ((), ())), preferred_element_type=jnp.float32)


def row_dot(a, b):
    return lax.dot_general(a, b, (((1,), (1,)), ((), ())), preferred_element_type=jnp.float32)


def kernel(
    q_ref,
    k_ref,
    v_ref,
    res_ref,
    gain_ref,
    ids_ref,
    gate_ref,
    win_in,
    wout_in,
    attn_ref,
    mix_ref,
    qs,
    kbuf,
    vbuf,
    row_max,
    row_sum,
    acc,
    select,
    route_hi,
    route_lo,
    normed,
    pack,
    win,
    wout,
    rows_own,
    rows_near,
    out_own,
    out_near,
    back_near,
    back_own,
    combined,
    up_send,
    up_recv,
    sib_send,
    sib_recv,
    wz_recv,
    wy_recv,
    wsib_recv,
    wsrc_send,
    wrel_send,
    wy_send,
    wsib_send,
    wload,
    x_send,
    x_recv,
    near_send,
    near_recv,
    yback_send,
    yback_recv,
    xback_send,
    xback_recv,
):
    ctx = lax.axis_index("ctx")
    spot = lax.axis_index("exp")
    plane = ctx // 2
    core = lax.rem(ctx, 2)
    x = spot // 8
    half = lax.rem(spot // 4, 2)
    y = lax.rem(spot, 4)
    odd = lax.rem(plane, 2)
    even_plane = odd == 0
    odd_plane = odd == 1

    sibling = device(plane, 1 - core, x, half, y)
    above = device(lax.rem(plane + 1, PLANES), core, x, half, y)
    across_y = device(plane, core, x, half, lax.rem(y + 2, 4))
    y_out = device(plane, core, x, half, lax.rem(y + 1 + 2 * core, 4))
    y_back = device(plane, core, x, half, lax.rem(y + 3 - 2 * core, 4))

    def plane_of(dz):
        return plane + dz * (1 - 2 * odd)

    barrier = pltpu.get_barrier_semaphore()

    def greet(target):
        pl.semaphore_signal(barrier, inc=1, device_id=target, device_id_type=MESH)

    def greet_all():
        greet(sibling)
        greet(device(lax.rem(plane + 2 * odd + PLANES - 1, PLANES), core, x, half, y))
        for dy in (1, 2, 3):
            greet(device(plane, core, x, half, lax.rem(y + dy, 4)))
        for dx, dz in NEAR_FIRST[1:]:
            greet(device(plane_of(dz), core, lax.rem(x + dx, 4), half, y))

        @pl.when(plane == 0)
        def _():
            greet(device(7, core, x, 1 - half, y))

        @pl.when(plane == 7)
        def _():
            greet(device(0, core, x, 1 - half, y))
            greet(device(1, core, x, 1 - half, y))
            greet(device(5, core, x, half, y))

        @pl.when(plane == 1)
        def _():
            greet(device(7, core, x, 1 - half, y))
            greet(device(3, core, x, half, y))

        @pl.when(plane == 5)
        def _():
            greet(device(7, core, x, half, y))

        @pl.when(plane == 3)
        def _():
            greet(device(1, core, x, half, y))

    greet_all()

    @pl.when(even_plane)
    def _():
        pltpu.make_async_copy(win_in, win.at[0], wload.at[0]).start()
        pltpu.make_async_copy(wout_in, wout.at[0], wload.at[1]).start()

    own_rows = pl.ds(pl.multiple_of(core * TOK, TOK), TOK)
    other_rows = pl.ds(pl.multiple_of((1 - core) * TOK, TOK), TOK)
    kbuf[plane, own_rows, :] = k_ref[...]
    vbuf[plane, own_rows, :] = v_ref[...]

    few = jnp.where((plane == 0) | (plane == 3) | (plane == 5), 1, 0)
    more = jnp.where(plane == 1, 2, jnp.where(plane == 7, 3, 0))
    pl.semaphore_wait(barrier, 12 + few + more)

    def kv_copy(which, chip, rows, send, recv, target):
        buf = kbuf if which == 0 else vbuf
        piece = buf.at[chip, rows, :]
        return pltpu.make_async_remote_copy(
            src_ref=piece,
            dst_ref=piece,
            send_sem=send.at[chip, which],
            recv_sem=recv.at[chip, which],
            device_id=target,
            device_id_type=MESH,
        )

    def up_copy(which, chip):
        return kv_copy(which, chip, own_rows, up_send, up_recv, above)

    def sib_copy(which, chip):
        return kv_copy(which, chip, own_rows, sib_send, sib_recv, sibling)

    def sib_arrival(which, chip):
        return kv_copy(which, chip, other_rows, sib_send, sib_recv, sibling)

    def spread(which, chip):
        @pl.when(plane < PLANES - 1)
        def _():
            up_copy(which, chip).start()

        sib_copy(which, chip).start()

    for which in (0, 1):
        spread(which, plane)

    def in_piece(ref, k):
        return ref.at[pl.ds(pl.multiple_of(core * 1024 + k * IN_ROWS, IN_ROWS), IN_ROWS), :]

    def out_piece(ref, k):
        return ref.at[pl.ds(pl.multiple_of(core * 96 + (k // 2) * OUT_ROWS, OUT_ROWS), OUT_ROWS), :]

    def has_out(k):
        return (lax.rem(k, 2) == 0) & (k < 2 * OUT_SUBS)

    def both_kinds(k, do):
        do(0, in_piece)

        @pl.when(has_out(k))
        def _():
            do(1, out_piece)

    def weight_ref(kind, slot):
        return win.at[slot] if kind == 0 else wout.at[slot]

    def weight_input(kind):
        return win_in if kind == 0 else wout_in

    def weight_copy(src, dst, send, recv, target):
        return pltpu.make_async_remote_copy(
            src_ref=src,
            dst_ref=dst,
            send_sem=send,
            recv_sem=recv,
            device_id=target,
            device_id_type=MESH,
        )

    def send_inputs(k):
        def one(kind, piece):
            source = piece(weight_input(kind), k)

            @pl.when(even_plane)
            def _():
                weight_copy(
                    source, piece(weight_ref(kind, 1), k), wy_send.at[kind], wy_recv.at[k, kind], across_y
                ).start()

            @pl.when(plane == 0)
            def _():
                weight_copy(
                    source,
                    piece(weight_ref(kind, 0), k),
                    wsrc_send.at[kind],
                    wz_recv.at[k, kind],
                    device(7, core, x, 1 - half, y),
                ).start()

            @pl.when(plane == 7)
            def _():
                weight_copy(
                    source,
                    piece(weight_ref(kind, 0), k),
                    wsrc_send.at[kind],
                    wz_recv.at[k, kind],
                    device(1, core, x, 1 - half, y),
                ).start()

        both_kinds(k, one)

    relay_target = device(jnp.where(plane == 7, 5, 3), core, x, half, y)
    relays = (plane == 7) | (plane == 1)

    def relay_z(k):
        def one(kind, piece):
            here = piece(weight_ref(kind, 0), k)
            weight_copy(here, here, wy_send.at[kind], wz_recv.at[k, kind], sibling).wait_recv()

            @pl.when(relays)
            def _():
                weight_copy(here, here, wrel_send.at[kind], wz_recv.at[k, kind], relay_target).start()

            weight_copy(
                here, piece(weight_ref(kind, 1), k), wy_send.at[kind], wy_recv.at[k, kind], across_y
            ).start()
            weight_copy(here, here, wsib_send.at[0, kind], wsib_recv.at[0, kind], sibling).start()

        @pl.when(odd_plane)
        def _():
            both_kinds(k, one)

    def relay_y(k):
        def one(kind, piece):
            here = piece(weight_ref(kind, 1), k)
            weight_copy(here, here, wy_send.at[kind], wy_recv.at[k, kind], sibling).wait_recv()
            weight_copy(here, here, wsib_send.at[1, kind], wsib_recv.at[1, kind], sibling).start()

        both_kinds(k, one)

    for head in range(HEADS):
        qs[head // 8, pl.ds((head % 8) * TOK, TOK), :] = q_ref[:, pl.ds(head * HD, HD)]

    column = lax.broadcasted_iota(jnp.int32, (TOK, TOK), 1)
    line = lax.broadcasted_iota(jnp.int32, (TOK, TOK), 0)
    expert_of = column // CAP
    slot_of = lax.rem(column, CAP)
    member = jnp.zeros((TOK, TOK), jnp.float32)
    route = jnp.zeros((TOK, TOK), jnp.float32)
    for k in range(8):
        match = ids_ref[:, pl.ds(k, 1)] == expert_of
        member = member + jnp.where(match, 1.0, 0.0)
        route = route + jnp.where(match, gate_ref[:, pl.ds(k, 1)], 0.0)
    earlier = jnp.where(column < line, 1.0, 0.0).astype(jnp.bfloat16)
    rank = jnp.dot(earlier, member.astype(jnp.bfloat16), preferred_element_type=jnp.float32)
    chosen = (member == 1.0) & (rank == slot_of.astype(jnp.float32))
    select[...] = jnp.where(chosen, 1.0, 0.0).astype(jnp.bfloat16)
    routed = jnp.where(chosen, route, 0.0)
    high = routed.astype(jnp.bfloat16)
    route_hi[...] = high
    route_lo[...] = (routed - high.astype(jnp.float32)).astype(jnp.bfloat16)

    scale = 1.0 / math.sqrt(HD)

    def attend(chip, first):
        for h in range(KV_HEADS):
            keys = kbuf[chip, :, pl.ds(h * HD, HD)]
            values = vbuf[chip, :, pl.ds(h * HD, HD)]
            for piece in range(4):
                span = pl.ds(piece * 256, 256)
                scores = row_dot(keys, qs[h, span, :]) * scale
                if first:
                    key_spot = lax.broadcasted_iota(jnp.int32, (256, 256), 0)
                    query_spot = lax.rem(lax.broadcasted_iota(jnp.int32, (256, 256), 1), TOK) + core * TOK
                    scores = jnp.where(key_spot <= query_spot, scores, MASKED)
                top = jnp.max(scores, axis=0, keepdims=True)
                if not first:
                    before = row_max[h, :, span]
                    top = jnp.maximum(before, top)
                weights = jnp.exp(scores - top)
                total = jnp.sum(weights, axis=0, keepdims=True)
                mixed = transposed_dot(values, weights.astype(jnp.bfloat16))
                if not first:
                    rescale = jnp.exp(before - top)
                    total = total + row_sum[h, :, span] * rescale
                    mixed = mixed + acc[h, :, span] * rescale
                row_max[h, :, span] = top
                row_sum[h, :, span] = total
                acc[h, :, span] = mixed

    for which in (0, 1):
        sib_arrival(which, plane).wait_recv()
    attend(plane, True)

    def step(t, carry):
        @pl.when(t < plane)
        def _():
            chip = plane - 1 - t
            for which in (0, 1):
                up_copy(which, chip).wait_recv()
                spread(which, chip)

        for k in (0, 1):
            send_inputs(2 * t + k)

        for k in (0, 1):
            relay_z(2 * t + k)

        @pl.when(t > 0)
        def _():
            for k in (0, 1):
                relay_y(2 * (t - 1) + k)

        @pl.when(t < plane)
        def _():
            chip = plane - 1 - t
            for which in (0, 1):
                sib_arrival(which, chip).wait_recv()
            attend(chip, False)

        return carry

    lax.fori_loop(0, 7, step, 0)

    for h in range(KV_HEADS):
        for g in range(8):
            span = pl.ds(g * TOK, TOK)
            done = acc[h, :, span] / row_sum[h, :, span]
            attn_ref[:, pl.ds((h * 8 + g) * HD, HD)] = done.T.astype(jnp.bfloat16)

    def norm_rows(i, carry):
        rows = pl.ds(pl.multiple_of(i * 16, 16), 16)
        stream = res_ref[rows, :].astype(jnp.float32) + attn_ref[rows, :].astype(jnp.float32)
        mean = jnp.mean(stream * stream, axis=-1, keepdims=True)
        normed[rows, :] = (stream * lax.rsqrt(mean + EPSILON) * gain_ref[...]).astype(jnp.bfloat16)
        return carry

    lax.fori_loop(0, TOK // 16, norm_rows, 0)
    for part in range(4):
        span = pl.ds(part * 512, 512)
        pack[:, :, span] = (
            transposed_dot(select[...], normed[:, span]).astype(jnp.bfloat16).reshape(8, CAP, 512)
        )

    my_slot = x * 2 + odd
    my_expert = x * 2 + lax.rem(half + odd, 2)

    def row_copy(src, dst, send, recv, target):
        return pltpu.make_async_remote_copy(
            src_ref=src, dst_ref=dst, send_sem=send, recv_sem=recv, device_id=target, device_id_type=MESH
        )

    def expert_at(dx, dz):
        other = plane_of(dz)
        return lax.rem(x + dx, 4) * 2 + lax.rem(half + lax.rem(other, 2), 2)

    def slot_from(dx, dz):
        return lax.rem(x + 4 - dx, 4) * 2 + lax.rem(plane_of(dz), 2)

    def dispatch(dx, dz):
        expert = expert_at(dx, dz)
        return row_copy(
            pack.at[expert],
            rows_own.at[my_slot],
            x_send.at[expert],
            x_recv.at[my_slot],
            device(plane_of(dz), core, lax.rem(x + dx, 4), half, y),
        )

    def arrival(dx, dz):
        slot = slot_from(dx, dz)
        return row_copy(pack.at[0], rows_own.at[slot], x_send.at[0], x_recv.at[slot], sibling)

    def forward(slot):
        return row_copy(rows_own.at[slot], rows_near.at[slot], near_send.at[slot], near_recv.at[slot], y_out)

    def return_y(slot):
        return row_copy(out_near.at[slot], back_near.at[slot], yback_send.at[slot], yback_recv.at[slot], y_back)

    def return_x(dx, dz):
        slot = slot_from(dx, dz)
        return row_copy(
            back_own.at[slot],
            combined.at[my_expert],
            xback_send.at[slot],
            xback_recv.at[my_expert],
            device(plane_of(dz), core, lax.rem(x + 4 - dx, 4), half, y),
        )

    def return_arrival(dx, dz):
        expert = expert_at(dx, dz)
        return row_copy(back_own.at[0], combined.at[expert], xback_send.at[0], xback_recv.at[expert], sibling)

    for dx, dz in NEAR_FIRST[1:]:
        dispatch(dx, dz).start()
    rows_own[my_slot] = pack[my_expert]
    forward(my_slot).start()

    for k in range(14, 16):
        send_inputs(jnp.int32(k))
    for k in range(14, 16):
        relay_z(jnp.int32(k))
    for k in range(12, 14):
        relay_y(jnp.int32(k))

    for dx, dz in NEAR_FIRST[1:]:
        arrival(dx, dz).wait_recv()
        forward(slot_from(dx, dz)).start()

    for k in range(14, 16):
        relay_y(jnp.int32(k))

    def half_in(ref, which):
        return ref.at[pl.ds(pl.multiple_of(which * 1024, 1024), 1024), :]

    def half_out(ref, which):
        return ref.at[pl.ds(pl.multiple_of(which * 96, 32), 96), :]

    def half_weight(kind, slot, which):
        return half_in(win.at[slot], which) if kind == 0 else half_out(wout.at[slot], which)

    @pl.when(even_plane)
    def _():
        pltpu.make_async_copy(win_in, win.at[0], wload.at[0]).wait()
        pltpu.make_async_copy(wout_in, wout.at[0], wload.at[1]).wait()

    def sib_weights(slot, kind):
        there = half_weight(kind, slot, 1 - core)
        return weight_copy(there, there, wsib_send.at[slot, kind], wsib_recv.at[slot, kind], sibling)

    for kind in (0, 1):

        @pl.when(odd_plane)
        def _():
            sib_weights(0, kind).wait_recv()

        sib_weights(1, kind).wait_recv()

    def ffn(rows, store):
        acts = []
        for slot in range(2):
            hidden = jnp.dot(rows, win[slot], preferred_element_type=jnp.float32)
            gate = hidden[:, :HID]
            acts.append((gate / (1.0 + jnp.exp(-gate)) * hidden[:, HID:]).astype(jnp.bfloat16))
        for part in range(4):
            span = pl.ds(part * 512, 512)
            made = jnp.dot(acts[0], wout[0, :, span], preferred_element_type=jnp.float32)
            made = made + jnp.dot(acts[1], wout[1, :, span], preferred_element_type=jnp.float32)
            store(span, made)

    def store_own(span, made):
        out_own[:, :, span] = made.reshape(8, CAP, 512)

    def store_near(span, made):
        out_near[:, :, span] = made.astype(jnp.bfloat16).reshape(8, CAP, 512)

    ffn(rows_own[...].reshape(TOK, D), store_own)

    for slot in range(8):
        row_copy(
            rows_own.at[slot], rows_near.at[slot], near_send.at[slot], near_recv.at[slot], y_out
        ).wait_recv()
    ffn(rows_near[...].reshape(TOK, D), store_near)
    for dx, dz in NEAR_FIRST[::-1]:
        return_y(slot_from(dx, dz)).start()

    for dx, dz in NEAR_FIRST[::-1]:
        slot = slot_from(dx, dz)
        return_y(slot).wait_recv()
        both = (out_own[slot] + back_near[slot].astype(jnp.float32)).astype(jnp.bfloat16)
        if (dx, dz) == (0, 0):
            combined[my_expert] = both
        else:
            back_own[slot] = both
            return_x(dx, dz).start()

    for dx, dz in NEAR_FIRST[1:]:
        return_arrival(dx, dz).wait_recv()

    for part in range(4):
        span = pl.ds(part * 512, 512)
        here = combined[:, :, span].reshape(TOK, 512)
        mixed = jnp.dot(route_hi[...], here, preferred_element_type=jnp.float32)
        mixed = mixed + jnp.dot(route_lo[...], here, preferred_element_type=jnp.float32)
        mix_ref[:, span] = mixed.astype(jnp.bfloat16)

    for dx, dz in NEAR_FIRST[1:]:
        dispatch(dx, dz).wait_send()
        return_x(dx, dz).wait_send()
    for slot in range(8):
        forward(slot).wait_send()
        return_y(slot).wait_send()

    def drain(s, carry):
        for which in (0, 1):

            @pl.when(plane < PLANES - 1)
            def _():
                up_copy(which, s).wait_send()

            sib_copy(which, s).wait_send()
        return carry

    lax.fori_loop(0, plane + 1, drain, 0)

    for kind in (0, 1):
        mine = half_weight(kind, 1, core)
        weight_copy(mine, mine, wy_send.at[kind], wsib_recv.at[1, kind], sibling).wait_send()
        weight_copy(mine, mine, wsib_send.at[1, kind], wsib_recv.at[1, kind], sibling).wait_send()

        @pl.when(odd_plane)
        def _():
            weight_copy(mine, mine, wsib_send.at[0, kind], wsib_recv.at[0, kind], sibling).wait_send()

        @pl.when((plane == 0) | (plane == 7))
        def _():
            weight_copy(mine, mine, wsrc_send.at[kind], wsib_recv.at[0, kind], sibling).wait_send()

        @pl.when(relays)
        def _():
            weight_copy(mine, mine, wrel_send.at[kind], wsib_recv.at[0, kind], sibling).wait_send()


def per_device(
    queries,
    key_states,
    value_states,
    residual,
    norm_gain,
    expert_ids,
    gate_weights,
    expert_in,
    expert_out,
):
    vmem = pl.BlockSpec(memory_space=pltpu.VMEM)
    anywhere = pl.BlockSpec(memory_space=pl.ANY)
    bf16, f32 = jnp.bfloat16, jnp.float32
    dma = pltpu.SemaphoreType.DMA
    rows = pltpu.VMEM((8, CAP, D), bf16)
    attention, mixed = pl.pallas_call(
        kernel,
        out_shape=(jax.ShapeDtypeStruct((TOK, D), bf16), jax.ShapeDtypeStruct((TOK, D), bf16)),
        in_specs=[vmem] * 7 + [anywhere] * 2,
        out_specs=(vmem, vmem),
        scratch_shapes=[
            pltpu.VMEM((KV_HEADS, 1024, HD), bf16),
            pltpu.VMEM((PLANES, 256, 256), bf16),
            pltpu.VMEM((PLANES, 256, 256), bf16),
            pltpu.VMEM((KV_HEADS, 1, 1024), f32),
            pltpu.VMEM((KV_HEADS, 1, 1024), f32),
            pltpu.VMEM((KV_HEADS, HD, 1024), f32),
            pltpu.VMEM((TOK, TOK), bf16),
            pltpu.VMEM((TOK, TOK), bf16),
            pltpu.VMEM((TOK, TOK), bf16),
            pltpu.VMEM((TOK, D), bf16),
            rows,
            pltpu.VMEM((2, D, 2 * HID), bf16),
            pltpu.VMEM((2, HID, D), bf16),
            rows,
            rows,
            pltpu.VMEM((8, CAP, D), f32),
            rows,
            rows,
            rows,
            rows,
            dma((PLANES, 2)),
            dma((PLANES, 2)),
            dma((PLANES, 2)),
            dma((PLANES, 2)),
            dma((SUBS, 2)),
            dma((SUBS, 2)),
            dma((2, 2)),
            dma((2,)),
            dma((2,)),
            dma((2,)),
            dma((2, 2)),
            dma((2,)),
            dma((8,)),
            dma((8,)),
            dma((8,)),
            dma((8,)),
            dma((8,)),
            dma((8,)),
            dma((8,)),
            dma((8,)),
        ],
        compiler_params=pltpu.CompilerParams(
            collective_id=0, has_side_effects=True, vmem_limit_bytes=48 << 20
        ),
    )(
        queries[0],
        key_states[0],
        value_states[0],
        residual[0],
        norm_gain[None],
        expert_ids[0],
        gate_weights[0],
        expert_in[0],
        expert_out[0],
    )
    return attention[None], mixed[None]


def solution(mesh):
    placed = P("exp", "ctx", None)
    return jax.shard_map(
        per_device,
        mesh=mesh,
        in_specs=(placed,) * 4 + (P(),) + (placed,) * 2 + (P("exp", None, None),) * 2,
        out_specs=(placed, placed),
        check_vma=False,
    )
```

```python
import functools
import math

import jax
import jax.numpy as jnp
from jax import lax
from jax.experimental import pallas as pl
from jax.experimental.pallas import tpu as pltpu
from jax.sharding import PartitionSpec as P

D = 2048
HEADS = 16
KV_HEADS = 2
HD = 128
TOK = 128
CAP = 16
HID = 192
PLANES = 8
SUBS = 16
IN_ROWS = 1024 // SUBS
OUT_SUBS = 6
OUT_ROWS = 16
EPSILON = 1e-06
MASKED = -1e30
MESH = pl.DeviceIdType.MESH
NEAR_FIRST = ((0, 0), (0, 1), (1, 0), (3, 0), (1, 1), (3, 1), (2, 0), (2, 1))


def device(plane, core, x, half, y):
    return (plane * 2 + core, x * 8 + half * 4 + y)


def transposed_dot(a, b):
    return lax.dot_general(a, b, (((0,), (0,)), ((), ())), preferred_element_type=jnp.float32)


def row_dot(a, b):
    return lax.dot_general(a, b, (((1,), (1,)), ((), ())), preferred_element_type=jnp.float32)


def kernel(
    q_ref,
    k_ref,
    v_ref,
    res_ref,
    gain_ref,
    ids_ref,
    gate_ref,
    win_in,
    wout_in,
    attn_ref,
    mix_ref,
    ids_v,
    gate_v,
    gain_v,
    res_v,
    qs,
    kbuf,
    vbuf,
    row_max,
    row_sum,
    acc,
    select,
    route_hi,
    route_lo,
    normed,
    pack,
    win,
    wout,
    rows_own,
    rows_near,
    out_own,
    out_near,
    back_near,
    back_own,
    combined,
    up_send,
    up_recv,
    sib_send,
    sib_recv,
    wz_recv,
    wy_recv,
    wsib_recv,
    wsrc_send,
    wrel_send,
    wy_send,
    wsib_send,
    wload,
    load,
    x_send,
    x_recv,
    near_send,
    near_recv,
    yback_send,
    yback_recv,
    xback_send,
    xback_recv,
):
    ctx = lax.axis_index("ctx")
    spot = lax.axis_index("exp")
    plane = ctx // 2
    core = lax.rem(ctx, 2)
    x = spot // 8
    half = lax.rem(spot // 4, 2)
    y = lax.rem(spot, 4)
    odd = lax.rem(plane, 2)
    even_plane = odd == 0
    odd_plane = odd == 1

    sibling = device(plane, 1 - core, x, half, y)
    above = device(lax.rem(plane + 1, PLANES), core, x, half, y)
    across_y = device(plane, core, x, half, lax.rem(y + 2, 4))
    y_out = device(plane, core, x, half, lax.rem(y + 1 + 2 * core, 4))
    y_back = device(plane, core, x, half, lax.rem(y + 3 - 2 * core, 4))

    def plane_of(dz):
        return plane + dz * (1 - 2 * odd)

    barrier = pltpu.get_barrier_semaphore()

    def greet(target):
        pl.semaphore_signal(barrier, inc=1, device_id=target, device_id_type=MESH)

    def greet_all():
        greet(sibling)
        greet(device(lax.rem(plane + 2 * odd + PLANES - 1, PLANES), core, x, half, y))
        for dy in (1, 2, 3):
            greet(device(plane, core, x, half, lax.rem(y + dy, 4)))
        for dx, dz in NEAR_FIRST[1:]:
            greet(device(plane_of(dz), core, lax.rem(x + dx, 4), half, y))

        @pl.when(plane == 0)
        def _():
            greet(device(7, core, x, 1 - half, y))

        @pl.when(plane == 7)
        def _():
            greet(device(0, core, x, 1 - half, y))
            greet(device(1, core, x, 1 - half, y))
            greet(device(5, core, x, half, y))

        @pl.when(plane == 1)
        def _():
            greet(device(7, core, x, 1 - half, y))
            greet(device(3, core, x, half, y))

        @pl.when(plane == 5)
        def _():
            greet(device(7, core, x, half, y))

        @pl.when(plane == 3)
        def _():
            greet(device(1, core, x, half, y))

    greet_all()

    own_rows = pl.ds(pl.multiple_of(core * TOK, TOK), TOK)
    other_rows = pl.ds(pl.multiple_of((1 - core) * TOK, TOK), TOK)
    k_load = pltpu.make_async_copy(k_ref, kbuf.at[plane, own_rows, :], load.at[0])
    v_load = pltpu.make_async_copy(v_ref, vbuf.at[plane, own_rows, :], load.at[1])
    k_load.start()
    v_load.start()
    q_loads = [
        pltpu.make_async_copy(
            q_ref.at[:, pl.ds(head * HD, HD)],
            qs.at[head // 8, pl.ds((head % 8) * TOK, TOK), :],
            load.at[6 + head],
        )
        for head in range(HEADS)
    ]
    small_loads = [
        pltpu.make_async_copy(ids_ref, ids_v, load.at[2]),
        pltpu.make_async_copy(gate_ref, gate_v, load.at[3]),
    ]
    late_loads = [
        pltpu.make_async_copy(gain_ref, gain_v, load.at[4]),
        pltpu.make_async_copy(res_ref, res_v, load.at[5]),
    ]
    for one_load in q_loads + small_loads + late_loads:
        one_load.start()

    @pl.when(even_plane)
    def _():
        pltpu.make_async_copy(win_in, win.at[0], wload.at[0]).start()
        pltpu.make_async_copy(wout_in, wout.at[0], wload.at[1]).start()

    k_load.wait()
    v_load.wait()
    few = jnp.where((plane == 0) | (plane == 3) | (plane == 5), 1, 0)
    more = jnp.where(plane == 1, 2, jnp.where(plane == 7, 3, 0))
    pl.semaphore_wait(barrier, 12 + few + more)

    def kv_copy(which, chip, rows, send, recv, target):
        buf = kbuf if which == 0 else vbuf
        piece = buf.at[chip, rows, :]
        return pltpu.make_async_remote_copy(
            src_ref=piece,
            dst_ref=piece,
            send_sem=send.at[chip, which],
            recv_sem=recv.at[chip, which],
            device_id=target,
            device_id_type=MESH,
        )

    def up_copy(which, chip):
        return kv_copy(which, chip, own_rows, up_send, up_recv, above)

    def sib_copy(which, chip):
        return kv_copy(which, chip, own_rows, sib_send, sib_recv, sibling)

    def sib_arrival(which, chip):
        return kv_copy(which, chip, other_rows, sib_send, sib_recv, sibling)

    def spread(which, chip):
        @pl.when(plane < PLANES - 1)
        def _():
            up_copy(which, chip).start()

        sib_copy(which, chip).start()

    for which in (0, 1):
        spread(which, plane)

    def in_piece(ref, k):
        return ref.at[pl.ds(pl.multiple_of(core * 1024 + k * IN_ROWS, IN_ROWS), IN_ROWS), :]

    def out_piece(ref, k):
        return ref.at[pl.ds(pl.multiple_of(core * 96 + (k // 2) * OUT_ROWS, OUT_ROWS), OUT_ROWS), :]

    def has_out(k):
        return (lax.rem(k, 2) == 0) & (k < 2 * OUT_SUBS)

    def both_kinds(k, do):
        do(0, in_piece)

        @pl.when(has_out(k))
        def _():
            do(1, out_piece)

    def weight_ref(kind, slot):
        return win.at[slot] if kind == 0 else wout.at[slot]

    def weight_input(kind):
        return win_in if kind == 0 else wout_in

    def weight_copy(src, dst, send, recv, target):
        return pltpu.make_async_remote_copy(
            src_ref=src,
            dst_ref=dst,
            send_sem=send,
            recv_sem=recv,
            device_id=target,
            device_id_type=MESH,
        )

    def send_across(k):
        def one(kind, piece):
            weight_copy(
                piece(weight_input(kind), k),
                piece(weight_ref(kind, 1), k),
                wy_send.at[kind],
                wy_recv.at[k, kind],
                across_y,
            ).start()

        @pl.when(even_plane)
        def _():
            both_kinds(k, one)

    source_target = device(jnp.where(plane == 0, 7, 1), core, x, 1 - half, y)
    sources = (plane == 0) | (plane == 7)

    def send_far(k):
        def one(kind, piece):
            weight_copy(
                piece(weight_input(kind), k),
                piece(weight_ref(kind, 0), k),
                wsrc_send.at[kind],
                wz_recv.at[k, kind],
                source_target,
            ).start()

        both_kinds(k, one)

    def far(k):
        @pl.when(sources)
        def _():
            send_far(k)

    relay_target = device(jnp.where(plane == 7, 5, 3), core, x, half, y)
    relays = (plane == 7) | (plane == 1)

    def relay_z(k):
        def one(kind, piece):
            here = piece(weight_ref(kind, 0), k)
            weight_copy(here, here, wy_send.at[kind], wz_recv.at[k, kind], sibling).wait_recv()

            @pl.when(relays)
            def _():
                weight_copy(here, here, wrel_send.at[kind], wz_recv.at[k, kind], relay_target).start()

            weight_copy(
                here, piece(weight_ref(kind, 1), k), wy_send.at[kind], wy_recv.at[k, kind], across_y
            ).start()
            weight_copy(here, here, wsib_send.at[0, kind], wsib_recv.at[0, kind], sibling).start()

        @pl.when(odd_plane & (k >= 0) & (k < SUBS))
        def _():
            both_kinds(k, one)

    def relay_y(k):
        def one(kind, piece):
            here = piece(weight_ref(kind, 1), k)
            weight_copy(here, here, wy_send.at[kind], wy_recv.at[k, kind], sibling).wait_recv()
            weight_copy(here, here, wsib_send.at[1, kind], wsib_recv.at[1, kind], sibling).start()

        @pl.when((k >= 0) & (k < SUBS))
        def _():
            both_kinds(k, one)

    for one_load in small_loads:
        one_load.wait()
    column = lax.broadcasted_iota(jnp.int32, (TOK, TOK), 1)
    line = lax.broadcasted_iota(jnp.int32, (TOK, TOK), 0)
    expert_of = line // CAP
    slot_of = lax.rem(line, CAP)
    member = jnp.zeros((TOK, TOK), jnp.float32)
    route = jnp.zeros((TOK, TOK), jnp.float32)
    for k in range(8):
        match = ids_v[pl.ds(k, 1), :] == expert_of
        member = member + jnp.where(match, 1.0, 0.0)
        route = route + jnp.where(match, gate_v[pl.ds(k, 1), :], 0.0)
    earlier = jnp.where(line < column, 1.0, 0.0).astype(jnp.bfloat16)
    rank = jnp.dot(member.astype(jnp.bfloat16), earlier, preferred_element_type=jnp.float32)
    chosen = (member == 1.0) & (rank == slot_of.astype(jnp.float32))
    select[...] = jnp.where(chosen, 1.0, 0.0).astype(jnp.bfloat16)
    routed = jnp.where(chosen, route, 0.0)
    high = routed.astype(jnp.bfloat16)
    route_hi[...] = high
    route_lo[...] = (routed - high.astype(jnp.float32)).astype(jnp.bfloat16)

    scale = 1.0 / math.sqrt(HD)

    def attend(chip, first):
        for h in range(KV_HEADS):
            keys = kbuf[chip, :, pl.ds(h * HD, HD)]
            values = vbuf[chip, :, pl.ds(h * HD, HD)]
            for piece in range(4):
                span = pl.ds(piece * 256, 256)
                scores = row_dot(keys, qs[h, span, :]) * scale
                if first:
                    key_spot = lax.broadcasted_iota(jnp.int32, (256, 256), 0)
                    query_spot = lax.rem(lax.broadcasted_iota(jnp.int32, (256, 256), 1), TOK) + core * TOK
                    scores = jnp.where(key_spot <= query_spot, scores, MASKED)
                top = jnp.max(scores, axis=0, keepdims=True)
                if not first:
                    before = row_max[h, :, span]
                    top = jnp.maximum(before, top)
                weights = jnp.exp(scores - top)
                total = jnp.sum(weights, axis=0, keepdims=True)
                mixed = transposed_dot(values, weights.astype(jnp.bfloat16))
                if not first:
                    rescale = jnp.exp(before - top)
                    total = total + row_sum[h, :, span] * rescale
                    mixed = mixed + acc[h, :, span] * rescale
                row_max[h, :, span] = top
                row_sum[h, :, span] = total
                acc[h, :, span] = mixed

    for one_load in q_loads:
        one_load.wait()
    for which in (0, 1):
        sib_arrival(which, plane).wait_recv()
    attend(plane, True)

    lag_z = jnp.where((plane == 1) | (plane == 7), 1, 3)
    lag_y = jnp.where(even_plane, 2, lag_z + 2)

    def step(t, carry):
        @pl.when(t < plane)
        def _():
            chip = plane - 1 - t
            for which in (0, 1):
                up_copy(which, chip).wait_recv()
                spread(which, chip)

        for k in (0, 1):
            send_across(2 * t + k)
            far(2 * t + k)
        for k in (0, 1):
            relay_z(2 * (t - lag_z) + k)
        for k in (0, 1):
            relay_y(2 * (t - lag_y) + k)

        @pl.when(t < plane)
        def _():
            chip = plane - 1 - t
            for which in (0, 1):
                sib_arrival(which, chip).wait_recv()
            attend(chip, False)

        return carry

    lax.fori_loop(0, 7, step, 0)

    for h in range(KV_HEADS):
        for g in range(8):
            span = pl.ds(g * TOK, TOK)
            done = acc[h, :, span] / row_sum[h, :, span]
            attn_ref[:, pl.ds((h * 8 + g) * HD, HD)] = done.T.astype(jnp.bfloat16)

    for one_load in late_loads:
        one_load.wait()

    def norm_rows(i, carry):
        rows = pl.ds(pl.multiple_of(i * 16, 16), 16)
        stream = res_v[rows, :].astype(jnp.float32) + attn_ref[rows, :].astype(jnp.float32)
        mean = jnp.mean(stream * stream, axis=-1, keepdims=True)
        normed[rows, :] = (stream * lax.rsqrt(mean + EPSILON) * gain_v[...]).astype(jnp.bfloat16)
        return carry

    lax.fori_loop(0, TOK // 16, norm_rows, 0)
    for part in range(4):
        span = pl.ds(part * 512, 512)
        pack[:, :, span] = (
            jnp.dot(select[...], normed[:, span], preferred_element_type=jnp.float32)
            .astype(jnp.bfloat16)
            .reshape(8, CAP, 512)
        )

    my_slot = x * 2 + odd
    my_expert = x * 2 + lax.rem(half + odd, 2)

    def row_copy(src, dst, send, recv, target):
        return pltpu.make_async_remote_copy(
            src_ref=src, dst_ref=dst, send_sem=send, recv_sem=recv, device_id=target, device_id_type=MESH
        )

    def expert_at(dx, dz):
        other = plane_of(dz)
        return lax.rem(x + dx, 4) * 2 + lax.rem(half + lax.rem(other, 2), 2)

    def slot_from(dx, dz):
        return lax.rem(x + 4 - dx, 4) * 2 + lax.rem(plane_of(dz), 2)

    def dispatch(dx, dz):
        expert = expert_at(dx, dz)
        return row_copy(
            pack.at[expert],
            rows_own.at[my_slot],
            x_send.at[expert],
            x_recv.at[my_slot],
            device(plane_of(dz), core, lax.rem(x + dx, 4), half, y),
        )

    def arrival(dx, dz):
        slot = slot_from(dx, dz)
        return row_copy(pack.at[0], rows_own.at[slot], x_send.at[0], x_recv.at[slot], sibling)

    def forward(slot):
        return row_copy(rows_own.at[slot], rows_near.at[slot], near_send.at[slot], near_recv.at[slot], y_out)

    def return_y(slot):
        return row_copy(out_near.at[slot], back_near.at[slot], yback_send.at[slot], yback_recv.at[slot], y_back)

    def return_x(dx, dz):
        slot = slot_from(dx, dz)
        return row_copy(
            back_own.at[slot],
            combined.at[my_expert],
            xback_send.at[slot],
            xback_recv.at[my_expert],
            device(plane_of(dz), core, lax.rem(x + 4 - dx, 4), half, y),
        )

    def return_arrival(dx, dz):
        expert = expert_at(dx, dz)
        return row_copy(back_own.at[0], combined.at[expert], xback_send.at[0], xback_recv.at[expert], sibling)

    for dx, dz in NEAR_FIRST[1:]:
        dispatch(dx, dz).start()
    rows_own[my_slot] = pack[my_expert]
    forward(my_slot).start()

    for k in (14, 15):
        send_across(jnp.int32(k))
        far(jnp.int32(k))
    z_done = 2 * (7 - lag_z)
    y_done = 2 * (7 - lag_y)
    for i, (dx, dz) in enumerate(NEAR_FIRST[1:]):
        relay_z(z_done + i)
        arrival(dx, dz).wait_recv()
        forward(slot_from(dx, dz)).start()
    relay_z(z_done + 7)

    def last_relays(k, carry):
        relay_y(k)
        return carry

    lax.fori_loop(y_done, SUBS, last_relays, 0)

    def half_in(ref, which):
        return ref.at[pl.ds(pl.multiple_of(which * 1024, 1024), 1024), :]

    def half_out(ref, which):
        return ref.at[pl.ds(pl.multiple_of(which * 96, 32), 96), :]

    def half_weight(kind, slot, which):
        return half_in(win.at[slot], which) if kind == 0 else half_out(wout.at[slot], which)

    @pl.when(even_plane)
    def _():
        pltpu.make_async_copy(win_in, win.at[0], wload.at[0]).wait()
        pltpu.make_async_copy(wout_in, wout.at[0], wload.at[1]).wait()

    def sib_weights(slot, kind):
        there = half_weight(kind, slot, 1 - core)
        return weight_copy(there, there, wsib_send.at[slot, kind], wsib_recv.at[slot, kind], sibling)

    for kind in (0, 1):

        @pl.when(odd_plane)
        def _():
            sib_weights(0, kind).wait_recv()

        sib_weights(1, kind).wait_recv()

    def ffn(rows, store):
        acts = []
        for slot in range(2):
            hidden = jnp.dot(rows, win[slot], preferred_element_type=jnp.float32)
            gate = hidden[:, :HID]
            acts.append((gate / (1.0 + jnp.exp(-gate)) * hidden[:, HID:]).astype(jnp.bfloat16))
        for part in range(4):
            span = pl.ds(part * 512, 512)
            made = jnp.dot(acts[0], wout[0, :, span], preferred_element_type=jnp.float32)
            made = made + jnp.dot(acts[1], wout[1, :, span], preferred_element_type=jnp.float32)
            store(span, made)

    def store_own(span, made):
        out_own[:, :, span] = made.reshape(8, CAP, 512)

    def store_near(span, made):
        out_near[:, :, span] = made.astype(jnp.bfloat16).reshape(8, CAP, 512)

    ffn(rows_own[...].reshape(TOK, D), store_own)

    for slot in range(8):
        row_copy(
            rows_own.at[slot], rows_near.at[slot], near_send.at[slot], near_recv.at[slot], y_out
        ).wait_recv()
    ffn(rows_near[...].reshape(TOK, D), store_near)
    for dx, dz in NEAR_FIRST[::-1]:
        return_y(slot_from(dx, dz)).start()

    for dx, dz in NEAR_FIRST[::-1]:
        slot = slot_from(dx, dz)
        return_y(slot).wait_recv()
        both = (out_own[slot] + back_near[slot].astype(jnp.float32)).astype(jnp.bfloat16)
        if (dx, dz) == (0, 0):
            combined[my_expert] = both
        else:
            back_own[slot] = both
            return_x(dx, dz).start()

    for dx, dz in NEAR_FIRST[1:]:
        return_arrival(dx, dz).wait_recv()

    for part in range(4):
        span = pl.ds(part * 512, 512)
        here = combined[:, :, span].reshape(TOK, 512)
        mixed = transposed_dot(route_hi[...], here)
        mixed = mixed + transposed_dot(route_lo[...], here)
        mix_ref[:, span] = mixed.astype(jnp.bfloat16)

    for dx, dz in NEAR_FIRST[1:]:
        dispatch(dx, dz).wait_send()
        return_x(dx, dz).wait_send()
    for slot in range(8):
        forward(slot).wait_send()
        return_y(slot).wait_send()

    def drain(s, carry):
        for which in (0, 1):

            @pl.when(plane < PLANES - 1)
            def _():
                up_copy(which, s).wait_send()

            sib_copy(which, s).wait_send()
        return carry

    lax.fori_loop(0, plane + 1, drain, 0)

    for kind in (0, 1):
        mine = half_weight(kind, 1, core)
        weight_copy(mine, mine, wy_send.at[kind], wsib_recv.at[1, kind], sibling).wait_send()
        weight_copy(mine, mine, wsib_send.at[1, kind], wsib_recv.at[1, kind], sibling).wait_send()

        @pl.when(odd_plane)
        def _():
            weight_copy(mine, mine, wsib_send.at[0, kind], wsib_recv.at[0, kind], sibling).wait_send()

        @pl.when(sources)
        def _():
            weight_copy(mine, mine, wsrc_send.at[kind], wsib_recv.at[0, kind], sibling).wait_send()

        @pl.when(relays)
        def _():
            weight_copy(mine, mine, wrel_send.at[kind], wsib_recv.at[0, kind], sibling).wait_send()


def per_device(
    queries,
    key_states,
    value_states,
    residual,
    norm_gain,
    expert_ids,
    gate_weights,
    expert_in,
    expert_out,
):
    vmem = pl.BlockSpec(memory_space=pltpu.VMEM)
    hbm = pl.BlockSpec(memory_space=pltpu.MemorySpace.HBM)
    bf16, f32 = jnp.bfloat16, jnp.float32
    dma = pltpu.SemaphoreType.DMA
    rows = pltpu.VMEM((8, CAP, D), bf16)
    attention, mixed = pl.pallas_call(
        kernel,
        out_shape=(jax.ShapeDtypeStruct((TOK, D), bf16), jax.ShapeDtypeStruct((TOK, D), bf16)),
        in_specs=[hbm] * 9,
        out_specs=(vmem, vmem),
        scratch_shapes=[
            pltpu.VMEM((8, TOK), jnp.int32),
            pltpu.VMEM((8, TOK), f32),
            pltpu.VMEM((1, D), f32),
            pltpu.VMEM((TOK, D), bf16),
            pltpu.VMEM((KV_HEADS, 1024, HD), bf16),
            pltpu.VMEM((PLANES, 256, 256), bf16),
            pltpu.VMEM((PLANES, 256, 256), bf16),
            pltpu.VMEM((KV_HEADS, 1, 1024), f32),
            pltpu.VMEM((KV_HEADS, 1, 1024), f32),
            pltpu.VMEM((KV_HEADS, HD, 1024), f32),
            pltpu.VMEM((TOK, TOK), bf16),
            pltpu.VMEM((TOK, TOK), bf16),
            pltpu.VMEM((TOK, TOK), bf16),
            pltpu.VMEM((TOK, D), bf16),
            rows,
            pltpu.VMEM((2, D, 2 * HID), bf16),
            pltpu.VMEM((2, HID, D), bf16),
            rows,
            rows,
            pltpu.VMEM((8, CAP, D), f32),
            rows,
            rows,
            rows,
            rows,
            dma((PLANES, 2)),
            dma((PLANES, 2)),
            dma((PLANES, 2)),
            dma((PLANES, 2)),
            dma((SUBS, 2)),
            dma((SUBS, 2)),
            dma((2, 2)),
            dma((2,)),
            dma((2,)),
            dma((2,)),
            dma((2, 2)),
            dma((2,)),
            dma((22,)),
            dma((8,)),
            dma((8,)),
            dma((8,)),
            dma((8,)),
            dma((8,)),
            dma((8,)),
            dma((8,)),
            dma((8,)),
        ],
        compiler_params=pltpu.CompilerParams(
            collective_id=0, has_side_effects=True, vmem_limit_bytes=60 << 20
        ),
    )(
        queries[0],
        key_states[0],
        value_states[0],
        residual[0],
        norm_gain[None],
        expert_ids[0].T,
        gate_weights[0].T,
        expert_in[0],
        expert_out[0],
    )
    return attention[None], mixed[None]


def solution(mesh):
    placed = P("exp", "ctx", None)
    return jax.shard_map(
        per_device,
        mesh=mesh,
        in_specs=(placed,) * 4 + (P(),) + (placed,) * 2 + (P("exp", None, None),) * 2,
        out_specs=(placed, placed),
        check_vma=False,
    )
```

```python
import functools
import math

import jax
import jax.numpy as jnp
from jax import lax
from jax.experimental import pallas as pl
from jax.experimental.pallas import tpu as pltpu
from jax.sharding import PartitionSpec as P

D = 2048
HEADS = 16
KV_HEADS = 2
HD = 128
TOK = 128
CAP = 16
HID = 192
PLANES = 8
SUBS = 16
IN_ROWS = 1024 // SUBS
OUT_SUBS = 6
OUT_ROWS = 16
EPSILON = 1e-06
MASKED = -1e30
MESH = pl.DeviceIdType.MESH
NEAR_FIRST = ((0, 0), (0, 1), (1, 0), (3, 0), (1, 1), (3, 1), (2, 0), (2, 1))


def device(plane, core, x, half, y):
    return (plane * 2 + core, x * 8 + half * 4 + y)


def transposed_dot(a, b):
    return lax.dot_general(a, b, (((0,), (0,)), ((), ())), preferred_element_type=jnp.float32)


def row_dot(a, b):
    return lax.dot_general(a, b, (((1,), (1,)), ((), ())), preferred_element_type=jnp.float32)


def kernel(
    q_ref,
    k_ref,
    v_ref,
    res_ref,
    gain_ref,
    ids_ref,
    gate_ref,
    win_in,
    wout_in,
    attn_ref,
    mix_ref,
    ids_v,
    gate_v,
    gain_v,
    res_v,
    qs,
    kbuf,
    vbuf,
    row_max,
    row_sum,
    acc,
    select,
    route_hi,
    route_lo,
    normed,
    pack,
    win,
    wout,
    rows_own,
    rows_near,
    out_own,
    out_near,
    back_near,
    back_own,
    combined,
    up_send,
    up_recv,
    sib_send,
    sib_recv,
    wz_recv,
    wy_recv,
    wsib_recv,
    wsrc_send,
    wrel_send,
    wy_send,
    wsib_send,
    wload,
    load,
    x_send,
    x_recv,
    near_send,
    near_recv,
    yback_send,
    yback_recv,
    xback_send,
    xback_recv,
):
    ctx = lax.axis_index("ctx")
    spot = lax.axis_index("exp")
    plane = ctx // 2
    core = lax.rem(ctx, 2)
    x = spot // 8
    half = lax.rem(spot // 4, 2)
    y = lax.rem(spot, 4)
    odd = lax.rem(plane, 2)
    even_plane = odd == 0
    odd_plane = odd == 1

    sibling = device(plane, 1 - core, x, half, y)
    above = device(lax.rem(plane + 1, PLANES), core, x, half, y)
    across_y = device(plane, core, x, half, lax.rem(y + 2, 4))
    y_out = device(plane, core, x, half, lax.rem(y + 1 + 2 * core, 4))
    y_back = device(plane, core, x, half, lax.rem(y + 3 - 2 * core, 4))

    def plane_of(dz):
        return plane + dz * (1 - 2 * odd)

    barrier = pltpu.get_barrier_semaphore()

    def greet(target):
        pl.semaphore_signal(barrier, inc=1, device_id=target, device_id_type=MESH)

    def greet_all():
        greet(sibling)
        greet(device(lax.rem(plane + 2 * odd + PLANES - 1, PLANES), core, x, half, y))
        for dy in (1, 2, 3):
            greet(device(plane, core, x, half, lax.rem(y + dy, 4)))
        for dx, dz in NEAR_FIRST[1:]:
            greet(device(plane_of(dz), core, lax.rem(x + dx, 4), half, y))

        @pl.when(plane == 0)
        def _():
            greet(device(7, core, x, 1 - half, y))

        @pl.when(plane == 7)
        def _():
            greet(device(0, core, x, 1 - half, y))
            greet(device(1, core, x, 1 - half, y))
            greet(device(5, core, x, half, y))

        @pl.when(plane == 1)
        def _():
            greet(device(7, core, x, 1 - half, y))
            greet(device(3, core, x, half, y))

        @pl.when(plane == 5)
        def _():
            greet(device(7, core, x, half, y))

        @pl.when(plane == 3)
        def _():
            greet(device(1, core, x, half, y))

    greet_all()

    own_rows = pl.ds(pl.multiple_of(core * TOK, TOK), TOK)
    other_rows = pl.ds(pl.multiple_of((1 - core) * TOK, TOK), TOK)
    k_load = pltpu.make_async_copy(k_ref, kbuf.at[plane, own_rows, :], load.at[0])
    v_load = pltpu.make_async_copy(v_ref, vbuf.at[plane, own_rows, :], load.at[1])
    k_load.start()
    v_load.start()
    q_loads = [
        pltpu.make_async_copy(
            q_ref.at[:, pl.ds(head * HD, HD)],
            qs.at[head // 8, pl.ds((head % 8) * TOK, TOK), :],
            load.at[6 + head],
        )
        for head in range(HEADS)
    ]
    small_loads = [
        pltpu.make_async_copy(ids_ref, ids_v, load.at[2]),
        pltpu.make_async_copy(gate_ref, gate_v, load.at[3]),
    ]
    late_loads = [
        pltpu.make_async_copy(gain_ref, gain_v, load.at[4]),
        pltpu.make_async_copy(res_ref, res_v, load.at[5]),
    ]
    for one_load in q_loads + small_loads + late_loads:
        one_load.start()

    @pl.when(even_plane)
    def _():
        pltpu.make_async_copy(win_in, win.at[0], wload.at[0]).start()
        pltpu.make_async_copy(wout_in, wout.at[0], wload.at[1]).start()

    k_load.wait()
    v_load.wait()
    few = jnp.where((plane == 0) | (plane == 3) | (plane == 5), 1, 0)
    more = jnp.where(plane == 1, 2, jnp.where(plane == 7, 3, 0))
    pl.semaphore_wait(barrier, 12 + few + more)

    def kv_copy(which, chip, rows, send, recv, target):
        buf = kbuf if which == 0 else vbuf
        piece = buf.at[chip, rows, :]
        return pltpu.make_async_remote_copy(
            src_ref=piece,
            dst_ref=piece,
            send_sem=send.at[chip, which],
            recv_sem=recv.at[chip, which],
            device_id=target,
            device_id_type=MESH,
        )

    def up_copy(which, chip):
        return kv_copy(which, chip, own_rows, up_send, up_recv, above)

    def sib_copy(which, chip):
        return kv_copy(which, chip, own_rows, sib_send, sib_recv, sibling)

    def sib_arrival(which, chip):
        return kv_copy(which, chip, other_rows, sib_send, sib_recv, sibling)

    def spread(which, chip):
        @pl.when(plane < PLANES - 1)
        def _():
            up_copy(which, chip).start()

        sib_copy(which, chip).start()

    for which in (0, 1):
        spread(which, plane)

    def in_piece(ref, k):
        return ref.at[pl.ds(pl.multiple_of(core * 1024 + k * IN_ROWS, IN_ROWS), IN_ROWS), :]

    def out_piece(ref, k):
        return ref.at[pl.ds(pl.multiple_of(core * 96 + (k // 2) * OUT_ROWS, OUT_ROWS), OUT_ROWS), :]

    def has_out(k):
        return (lax.rem(k, 2) == 0) & (k < 2 * OUT_SUBS)

    def both_kinds(k, do):
        do(0, in_piece)

        @pl.when(has_out(k))
        def _():
            do(1, out_piece)

    def weight_ref(kind, slot):
        return win.at[slot] if kind == 0 else wout.at[slot]

    def weight_input(kind):
        return win_in if kind == 0 else wout_in

    def weight_copy(src, dst, send, recv, target):
        return pltpu.make_async_remote_copy(
            src_ref=src,
            dst_ref=dst,
            send_sem=send,
            recv_sem=recv,
            device_id=target,
            device_id_type=MESH,
        )

    def send_across(k):
        def one(kind, piece):
            weight_copy(
                piece(weight_input(kind), k),
                piece(weight_ref(kind, 1), k),
                wy_send.at[kind],
                wy_recv.at[k, kind],
                across_y,
            ).start()

        @pl.when(even_plane)
        def _():
            both_kinds(k, one)

    source_target = device(jnp.where(plane == 0, 7, 1), core, x, 1 - half, y)
    sources = (plane == 0) | (plane == 7)

    def send_far(k):
        def one(kind, piece):
            weight_copy(
                piece(weight_input(kind), k),
                piece(weight_ref(kind, 0), k),
                wsrc_send.at[kind],
                wz_recv.at[k, kind],
                source_target,
            ).start()

        both_kinds(k, one)

    def far(k):
        @pl.when(sources)
        def _():
            send_far(k)

    relay_target = device(jnp.where(plane == 7, 5, 3), core, x, half, y)
    relays = (plane == 7) | (plane == 1)

    def relay_z(k):
        def one(kind, piece):
            here = piece(weight_ref(kind, 0), k)
            weight_copy(here, here, wy_send.at[kind], wz_recv.at[k, kind], sibling).wait_recv()

            @pl.when(relays)
            def _():
                weight_copy(here, here, wrel_send.at[kind], wz_recv.at[k, kind], relay_target).start()

            weight_copy(
                here, piece(weight_ref(kind, 1), k), wy_send.at[kind], wy_recv.at[k, kind], across_y
            ).start()
            weight_copy(here, here, wsib_send.at[0, kind], wsib_recv.at[0, kind], sibling).start()

        @pl.when(odd_plane & (k >= 0) & (k < SUBS))
        def _():
            both_kinds(k, one)

    def relay_y(k):
        def one(kind, piece):
            here = piece(weight_ref(kind, 1), k)
            weight_copy(here, here, wy_send.at[kind], wy_recv.at[k, kind], sibling).wait_recv()
            weight_copy(here, here, wsib_send.at[1, kind], wsib_recv.at[1, kind], sibling).start()

        @pl.when((k >= 0) & (k < SUBS))
        def _():
            both_kinds(k, one)

    for one_load in small_loads:
        one_load.wait()
    column = lax.broadcasted_iota(jnp.int32, (TOK, TOK), 1)
    line = lax.broadcasted_iota(jnp.int32, (TOK, TOK), 0)
    expert_of = line // CAP
    slot_of = lax.rem(line, CAP)
    member = jnp.zeros((TOK, TOK), jnp.float32)
    route = jnp.zeros((TOK, TOK), jnp.float32)
    for k in range(8):
        match = ids_v[pl.ds(k, 1), :] == expert_of
        member = member + jnp.where(match, 1.0, 0.0)
        route = route + jnp.where(match, gate_v[pl.ds(k, 1), :], 0.0)
    earlier = jnp.where(line < column, 1.0, 0.0).astype(jnp.bfloat16)
    rank = jnp.dot(member.astype(jnp.bfloat16), earlier, preferred_element_type=jnp.float32)
    chosen = (member == 1.0) & (rank == slot_of.astype(jnp.float32))
    select[...] = jnp.where(chosen, 1.0, 0.0).astype(jnp.bfloat16)
    routed = jnp.where(chosen, route, 0.0)
    high = routed.astype(jnp.bfloat16)
    route_hi[...] = high
    route_lo[...] = (routed - high.astype(jnp.float32)).astype(jnp.bfloat16)

    scale = 1.0 / math.sqrt(HD)

    def attend(chip, first):
        for h in range(KV_HEADS):
            keys = kbuf[chip, :, pl.ds(h * HD, HD)]
            values = vbuf[chip, :, pl.ds(h * HD, HD)]
            for piece in range(4):
                span = pl.ds(piece * 256, 256)
                scores = row_dot(keys, qs[h, span, :]) * scale
                if first:
                    key_spot = lax.broadcasted_iota(jnp.int32, (256, 256), 0)
                    query_spot = lax.rem(lax.broadcasted_iota(jnp.int32, (256, 256), 1), TOK) + core * TOK
                    scores = jnp.where(key_spot <= query_spot, scores, MASKED)
                top = jnp.max(scores, axis=0, keepdims=True)
                if not first:
                    before = row_max[h, :, span]
                    top = jnp.maximum(before, top)
                weights = jnp.exp(scores - top)
                total = jnp.sum(weights, axis=0, keepdims=True)
                mixed = transposed_dot(values, weights.astype(jnp.bfloat16))
                if not first:
                    rescale = jnp.exp(before - top)
                    total = total + row_sum[h, :, span] * rescale
                    mixed = mixed + acc[h, :, span] * rescale
                row_max[h, :, span] = top
                row_sum[h, :, span] = total
                acc[h, :, span] = mixed

    for one_load in q_loads:
        one_load.wait()
    for which in (0, 1):
        sib_arrival(which, plane).wait_recv()
    attend(plane, True)

    lag_z = jnp.where((plane == 1) | (plane == 7), 1, 3)
    lag_y = jnp.where(even_plane, 2, lag_z + 2)

    def step(t, carry):
        @pl.when(t < plane)
        def _():
            chip = plane - 1 - t
            for which in (0, 1):
                up_copy(which, chip).wait_recv()
                spread(which, chip)

        for k in (0, 1):
            send_across(2 * t + k)
            far(2 * t + k)
        for k in (0, 1):
            relay_z(2 * (t - lag_z) + k)
        for k in (0, 1):
            relay_y(2 * (t - lag_y) + k)

        @pl.when(t < plane)
        def _():
            chip = plane - 1 - t
            for which in (0, 1):
                sib_arrival(which, chip).wait_recv()
            attend(chip, False)

        return carry

    lax.fori_loop(0, 7, step, 0)

    for k in (14, 15):
        send_across(jnp.int32(k))
        far(jnp.int32(k))

    for h in range(KV_HEADS):
        for g in range(8):
            span = pl.ds(g * TOK, TOK)
            done = acc[h, :, span] / row_sum[h, :, span]
            attn_ref[:, pl.ds((h * 8 + g) * HD, HD)] = done.T.astype(jnp.bfloat16)

    for one_load in late_loads:
        one_load.wait()

    def norm_rows(i, carry):
        rows = pl.ds(pl.multiple_of(i * 16, 16), 16)
        stream = res_v[rows, :].astype(jnp.float32) + attn_ref[rows, :].astype(jnp.float32)
        mean = jnp.mean(stream * stream, axis=-1, keepdims=True)
        normed[rows, :] = (stream * lax.rsqrt(mean + EPSILON) * gain_v[...]).astype(jnp.bfloat16)
        return carry

    lax.fori_loop(0, TOK // 16, norm_rows, 0)
    for part in range(4):
        span = pl.ds(part * 512, 512)
        pack[:, :, span] = (
            jnp.dot(select[...], normed[:, span], preferred_element_type=jnp.float32)
            .astype(jnp.bfloat16)
            .reshape(8, CAP, 512)
        )

    my_slot = x * 2 + odd
    my_expert = x * 2 + lax.rem(half + odd, 2)

    def row_copy(src, dst, send, recv, target):
        return pltpu.make_async_remote_copy(
            src_ref=src, dst_ref=dst, send_sem=send, recv_sem=recv, device_id=target, device_id_type=MESH
        )

    def expert_at(dx, dz):
        other = plane_of(dz)
        return lax.rem(x + dx, 4) * 2 + lax.rem(half + lax.rem(other, 2), 2)

    def slot_from(dx, dz):
        return lax.rem(x + 4 - dx, 4) * 2 + lax.rem(plane_of(dz), 2)

    def dispatch(dx, dz):
        expert = expert_at(dx, dz)
        return row_copy(
            pack.at[expert],
            rows_own.at[my_slot],
            x_send.at[expert],
            x_recv.at[my_slot],
            device(plane_of(dz), core, lax.rem(x + dx, 4), half, y),
        )

    def arrival(dx, dz):
        slot = slot_from(dx, dz)
        return row_copy(pack.at[0], rows_own.at[slot], x_send.at[0], x_recv.at[slot], sibling)

    def forward(slot):
        return row_copy(rows_own.at[slot], rows_near.at[slot], near_send.at[slot], near_recv.at[slot], y_out)

    def return_y(slot):
        return row_copy(out_near.at[slot], back_near.at[slot], yback_send.at[slot], yback_recv.at[slot], y_back)

    def return_x(dx, dz):
        slot = slot_from(dx, dz)
        return row_copy(
            back_own.at[slot],
            combined.at[my_expert],
            xback_send.at[slot],
            xback_recv.at[my_expert],
            device(plane_of(dz), core, lax.rem(x + 4 - dx, 4), half, y),
        )

    def return_arrival(dx, dz):
        expert = expert_at(dx, dz)
        return row_copy(back_own.at[0], combined.at[expert], xback_send.at[0], xback_recv.at[expert], sibling)

    for dx, dz in NEAR_FIRST[1:]:
        dispatch(dx, dz).start()
    rows_own[my_slot] = pack[my_expert]
    forward(my_slot).start()

    z_done = 2 * (7 - lag_z)
    y_done = 2 * (7 - lag_y)
    for i, (dx, dz) in enumerate(NEAR_FIRST[1:]):
        relay_z(z_done + i)
        arrival(dx, dz).wait_recv()
        forward(slot_from(dx, dz)).start()
    relay_z(z_done + 7)

    def last_relays(k, carry):
        relay_y(k)
        return carry

    lax.fori_loop(y_done, SUBS, last_relays, 0)

    def half_in(ref, which):
        return ref.at[pl.ds(pl.multiple_of(which * 1024, 1024), 1024), :]

    def half_out(ref, which):
        return ref.at[pl.ds(pl.multiple_of(which * 96, 32), 96), :]

    def half_weight(kind, slot, which):
        return half_in(win.at[slot], which) if kind == 0 else half_out(wout.at[slot], which)

    @pl.when(even_plane)
    def _():
        pltpu.make_async_copy(win_in, win.at[0], wload.at[0]).wait()
        pltpu.make_async_copy(wout_in, wout.at[0], wload.at[1]).wait()

    def sib_weights(slot, kind):
        there = half_weight(kind, slot, 1 - core)
        return weight_copy(there, there, wsib_send.at[slot, kind], wsib_recv.at[slot, kind], sibling)

    for kind in (0, 1):

        @pl.when(odd_plane)
        def _():
            sib_weights(0, kind).wait_recv()

        sib_weights(1, kind).wait_recv()

    def ffn(rows, store):
        acts = []
        for slot in range(2):
            hidden = jnp.dot(rows, win[slot], preferred_element_type=jnp.float32)
            gate = hidden[:, :HID]
            acts.append((gate / (1.0 + jnp.exp(-gate)) * hidden[:, HID:]).astype(jnp.bfloat16))
        for part in range(4):
            span = pl.ds(part * 512, 512)
            made = jnp.dot(acts[0], wout[0, :, span], preferred_element_type=jnp.float32)
            made = made + jnp.dot(acts[1], wout[1, :, span], preferred_element_type=jnp.float32)
            store(span, made)

    def store_own(span, made):
        out_own[:, :, span] = made.reshape(8, CAP, 512)

    def store_near(span, made):
        out_near[:, :, span] = made.astype(jnp.bfloat16).reshape(8, CAP, 512)

    for slot in range(8):
        row_copy(
            rows_own.at[slot], rows_near.at[slot], near_send.at[slot], near_recv.at[slot], y_out
        ).wait_recv()
    ffn(rows_near[...].reshape(TOK, D), store_near)
    for dx, dz in NEAR_FIRST[::-1]:
        return_y(slot_from(dx, dz)).start()
    ffn(rows_own[...].reshape(TOK, D), store_own)

    for dx, dz in NEAR_FIRST[::-1]:
        slot = slot_from(dx, dz)
        return_y(slot).wait_recv()
        both = (out_own[slot] + back_near[slot].astype(jnp.float32)).astype(jnp.bfloat16)
        if (dx, dz) == (0, 0):
            combined[my_expert] = both
        else:
            back_own[slot] = both
            return_x(dx, dz).start()

    for dx, dz in NEAR_FIRST[1:]:
        return_arrival(dx, dz).wait_recv()

    for part in range(4):
        span = pl.ds(part * 512, 512)
        here = combined[:, :, span].reshape(TOK, 512)
        mixed = transposed_dot(route_hi[...], here)
        mixed = mixed + transposed_dot(route_lo[...], here)
        mix_ref[:, span] = mixed.astype(jnp.bfloat16)

    for dx, dz in NEAR_FIRST[1:]:
        dispatch(dx, dz).wait_send()
        return_x(dx, dz).wait_send()
    for slot in range(8):
        forward(slot).wait_send()
        return_y(slot).wait_send()

    def drain(s, carry):
        for which in (0, 1):

            @pl.when(plane < PLANES - 1)
            def _():
                up_copy(which, s).wait_send()

            sib_copy(which, s).wait_send()
        return carry

    lax.fori_loop(0, plane + 1, drain, 0)

    for kind in (0, 1):
        mine = half_weight(kind, 1, core)
        weight_copy(mine, mine, wy_send.at[kind], wsib_recv.at[1, kind], sibling).wait_send()
        weight_copy(mine, mine, wsib_send.at[1, kind], wsib_recv.at[1, kind], sibling).wait_send()

        @pl.when(odd_plane)
        def _():
            weight_copy(mine, mine, wsib_send.at[0, kind], wsib_recv.at[0, kind], sibling).wait_send()

        @pl.when(sources)
        def _():
            weight_copy(mine, mine, wsrc_send.at[kind], wsib_recv.at[0, kind], sibling).wait_send()

        @pl.when(relays)
        def _():
            weight_copy(mine, mine, wrel_send.at[kind], wsib_recv.at[0, kind], sibling).wait_send()


def per_device(
    queries,
    key_states,
    value_states,
    residual,
    norm_gain,
    expert_ids,
    gate_weights,
    expert_in,
    expert_out,
):
    vmem = pl.BlockSpec(memory_space=pltpu.VMEM)
    hbm = pl.BlockSpec(memory_space=pltpu.MemorySpace.HBM)
    bf16, f32 = jnp.bfloat16, jnp.float32
    dma = pltpu.SemaphoreType.DMA
    rows = pltpu.VMEM((8, CAP, D), bf16)
    attention, mixed = pl.pallas_call(
        kernel,
        out_shape=(jax.ShapeDtypeStruct((TOK, D), bf16), jax.ShapeDtypeStruct((TOK, D), bf16)),
        in_specs=[hbm] * 9,
        out_specs=(vmem, vmem),
        scratch_shapes=[
            pltpu.VMEM((8, TOK), jnp.int32),
            pltpu.VMEM((8, TOK), f32),
            pltpu.VMEM((1, D), f32),
            pltpu.VMEM((TOK, D), bf16),
            pltpu.VMEM((KV_HEADS, 1024, HD), bf16),
            pltpu.VMEM((PLANES, 256, 256), bf16),
            pltpu.VMEM((PLANES, 256, 256), bf16),
            pltpu.VMEM((KV_HEADS, 1, 1024), f32),
            pltpu.VMEM((KV_HEADS, 1, 1024), f32),
            pltpu.VMEM((KV_HEADS, HD, 1024), f32),
            pltpu.VMEM((TOK, TOK), bf16),
            pltpu.VMEM((TOK, TOK), bf16),
            pltpu.VMEM((TOK, TOK), bf16),
            pltpu.VMEM((TOK, D), bf16),
            rows,
            pltpu.VMEM((2, D, 2 * HID), bf16),
            pltpu.VMEM((2, HID, D), bf16),
            rows,
            rows,
            pltpu.VMEM((8, CAP, D), f32),
            rows,
            rows,
            rows,
            rows,
            dma((PLANES, 2)),
            dma((PLANES, 2)),
            dma((PLANES, 2)),
            dma((PLANES, 2)),
            dma((SUBS, 2)),
            dma((SUBS, 2)),
            dma((2, 2)),
            dma((2,)),
            dma((2,)),
            dma((2,)),
            dma((2, 2)),
            dma((2,)),
            dma((22,)),
            dma((8,)),
            dma((8,)),
            dma((8,)),
            dma((8,)),
            dma((8,)),
            dma((8,)),
            dma((8,)),
            dma((8,)),
        ],
        compiler_params=pltpu.CompilerParams(
            collective_id=0, has_side_effects=True, vmem_limit_bytes=60 << 20
        ),
    )(
        queries[0],
        key_states[0],
        value_states[0],
        residual[0],
        norm_gain[None],
        expert_ids[0].T,
        gate_weights[0].T,
        expert_in[0],
        expert_out[0],
    )
    return attention[None], mixed[None]


def solution(mesh):
    placed = P("exp", "ctx", None)
    return jax.shard_map(
        per_device,
        mesh=mesh,
        in_specs=(placed,) * 4 + (P(),) + (placed,) * 2 + (P("exp", None, None),) * 2,
        out_specs=(placed, placed),
        check_vma=False,
    )
```
